32 devices in a mesh: dp: 16 (over z, y, core), mp: 2 (over x).
Axes of the slice: x: 2, y: 2, z: 4, core: 2. Of those that a mesh axis runs over, the one named last changes fastest.
Arguments:
- x_in: bfloat16 [2, 8192, 1024], P(None, 'dp'), may hold values from -6 to 6
- cotangent: bfloat16 [2, 8192, 1024], P(None, 'dp'), may hold values from -6 to 6
- positions: int32 [2, 8192], P(None, 'dp'), may hold values from -1 to 511, as said below
- norm1_gain: bfloat16 [1024], P('dp'), may hold values from 0.5 to 1.5
- w_z: bfloat16 [1024, 1536], P('dp', 'mp'), may hold values from -0.1875 to 0.1875
- w_x: bfloat16 [1024, 1536], P('dp', 'mp'), may hold values from -0.1875 to 0.1875
- w_dt: bfloat16 [1024, 24], P('dp', 'mp'), may hold values from -0.1875 to 0.1875
- w_q: bfloat16 [1024, 512], P('dp', 'mp'), may hold values from -0.1875 to 0.1875
- w_k: bfloat16 [1024, 128], P('dp', 'mp'), may hold values from -0.1875 to 0.1875
- w_v: bfloat16 [1024, 128], P('dp', 'mp'), may hold values from -0.1875 to 0.1875
- w_bc: bfloat16 [1024, 256], P(('dp', 'mp')), may hold values from -0.1875 to 0.1875
- conv_x_w: bfloat16 [4, 1536], P(None, 'mp'), may hold values from -3 to 3
- conv_x_b: bfloat16 [1536], P('mp'), may hold values from -3 to 3
- conv_bc_w: bfloat16 [4, 256], P(None, ('dp', 'mp')), may hold values from -3 to 3
- conv_bc_b: bfloat16 [256], P(('dp', 'mp')), may hold values from -3 to 3
- a_log: float32 [24], P('mp'), may hold values from -4 to 0.5
- dt_bias: float32 [24], P('mp'), may hold values from -6 to -2
- d_skip: float32 [24], P('mp'), may hold values from 0.5 to 1.5
- w_o: bfloat16 [512, 1024], P('mp', 'dp'), may hold values from -1 to 1
- w_out: bfloat16 [1536, 1024], P('mp', 'dp'), may hold values from -0.15625 to 0.15625
- norm2_gain: bfloat16 [1024], P('dp'), may hold values from 0.5 to 1.5
- w_gate: bfloat16 [1024, 2048], P('dp', 'mp'), may hold values from -0.1875 to 0.1875
- w_up: bfloat16 [1024, 2048], P('dp', 'mp'), may hold values from -0.1875 to 0.1875
- w_down: bfloat16 [2048, 1024], P('mp', 'dp'), may hold values from -0.25 to 0.25
Outputs:
- out: float32 [2, 8192, 1024], P(None, 'dp')
- grad_x: float32 [2, 8192, 1024], P(None, 'dp')
- g_norm1_gain: float32 [1024], P('dp')
- g_w_z: float32 [1024, 1536], P('dp', 'mp')
- g_w_x: float32 [1024, 1536], P('dp', 'mp')
- g_w_dt: float32 [1024, 24], P('dp', 'mp')
- g_w_q: float32 [1024, 512], P('dp', 'mp')
- g_w_k: float32 [1024, 128], P('dp', 'mp')
- g_w_v: float32 [1024, 128], P('dp', 'mp')
- g_w_bc: float32 [1024, 256], P(('dp', 'mp'))
- g_conv_x_w: float32 [4, 1536], P(None, 'mp')
- g_conv_x_b: float32 [1536], P('mp')
- g_conv_bc_w: float32 [4, 256], P(None, ('dp', 'mp'))
- g_conv_bc_b: float32 [256], P(('dp', 'mp'))
- g_a_log: float32 [24], P('mp')
- g_dt_bias: float32 [24], P('mp')
- g_d_skip: float32 [24], P('mp')
- g_w_o: float32 [512, 1024], P('mp', 'dp')
- g_w_out: float32 [1536, 1024], P('mp', 'dp')
- g_norm2_gain: float32 [1024], P('dp')
- g_w_gate: float32 [1024, 2048], P('dp', 'mp')
- g_w_up: float32 [1024, 2048], P('dp', 'mp')
- g_w_down: float32 [2048, 1024], P('mp', 'dp')
The draws below stay inside these ranges and needn't reach their ends.
Inputs may be any that keep to these rules, and one draw needn't show every extreme that they name: `positions`: within each aligned block of 512 rows, live rows come first and -1 marks the empty rows after them; a sequence's rows carry 0, 1, 2, ... in order, so 0 starts a new sequence; in some block all 512 rows hold one sequence.
All inputs are finite; a program needn't handle non-finite values.
Results may differ from the reference program's by a relative error of at most 0.015.
Values may be sent and summed in bfloat16 or wider, within the bound.
A program may use at most 192 MiB of HBM per device.

```python
import math
import jax
import jax.numpy as jnp
from jax import lax

D = 1024
MHEADS = 24
MHEAD_DIM = 64
STATE = 128
CONV = 4
QHEADS = 8
KVHEADS = 2
HEAD_DIM = 64
FF = 2048
SLOTS = 512
MB = 2
DSSM = 1536
ROWS = 8192
N_MP = 2


def draw_positions(key, part):
    buffer_count = MB * (ROWS // SLOTS)
    live_key, full_key, start_key = jax.random.split(key, 3)
    live_count = jax.random.randint(live_key, (buffer_count, 1), SLOTS // 8, 7 * SLOTS // 8 + 1)
    full_buffer = jax.random.randint(full_key, (), 0, buffer_count)
    buffer_index = jnp.arange(buffer_count, dtype=jnp.int32)[:, None]
    slot_index = jnp.arange(SLOTS, dtype=jnp.int32)[None, :]
    live_count = jnp.where(buffer_index == full_buffer, SLOTS, live_count)
    starting = jax.random.randint(start_key, (buffer_count, SLOTS), 0, max(SLOTS // 4, 2)) == 0
    starting = starting & (buffer_index != full_buffer) | (slot_index == 0)
    last_start = lax.cummax(jnp.where(starting, slot_index, 0), axis=1)
    placed = jnp.where(slot_index < live_count, slot_index - last_start, -1)
    return placed.astype(jnp.int32).reshape(MB, ROWS)


def levels(own_key, extent, pieces, low, largest):
    loudness = 1.0
    for dim, shards_of in pieces:
        steps = jax.random.uniform(jax.random.fold_in(jax.random.fold_in(own_key, 6), dim), (shards_of,), jnp.float32, low / len(pieces), largest / len(pieces))
        loudness = loudness * jnp.repeat(jnp.exp(steps), extent[dim] // shards_of).reshape((-1,) + (1,) * (len(extent) - 1 - dim))
    return loudness


def noise(own_key, shape, spread, bound, shards=(), held_as=jnp.bfloat16):
    factor_of = levels(own_key, shape, shards, -0.22, 0.18) if shards else 1.0
    drawn = jax.random.normal(own_key, shape, jnp.float32) * spread * factor_of
    return jnp.minimum(jnp.maximum(drawn, -bound), bound).astype(held_as)


def setup_inputs(seed: int = 0) -> dict:
    keys = jax.random.split(jax.random.key(seed), 25)
    x_in = noise(keys[0], (MB, ROWS, D), 1.0, 6.0, ((1, 16),))
    cotangent = noise(keys[1], (MB, ROWS, D), 1.0, 6.0, ((1, 16),))
    positions = draw_positions(jax.random.fold_in(keys[24], 71), 0)
    norm1_gain = jnp.clip(1.0 + 0.1 * jax.random.normal(keys[3], (D,), jnp.float32), 0.5, 1.5).astype(jnp.bfloat16)
    w_z = noise(keys[4], (D, DSSM), D ** -0.5, 0.1875, ((0, 16), (1, 2)))
    w_x = noise(keys[5], (D, DSSM), D ** -0.5, 0.1875, ((0, 16), (1, 2)))
    w_dt = noise(keys[6], (D, MHEADS), D ** -0.5, 0.1875, ((0, 16), (1, 2)))
    w_q = noise(keys[7], (D, QHEADS * HEAD_DIM), D ** -0.5, 0.1875, ((0, 16), (1, 2)))
    w_k = noise(keys[8], (D, KVHEADS * HEAD_DIM), D ** -0.5, 0.1875, ((0, 16), (1, 2)))
    w_v = noise(keys[9], (D, KVHEADS * HEAD_DIM), D ** -0.5, 0.1875, ((0, 16), (1, 2)))
    w_bc = noise(keys[10], (D, 2 * STATE), D ** -0.5, 0.1875, ((0, 32),))
    conv_x_w = noise(keys[11], (CONV, DSSM), 0.5, 3.0, ((1, 2),))
    conv_x_b = noise(keys[12], (DSSM,), 0.5, 3.0, ((0, 2),))
    conv_bc_w = noise(keys[13], (CONV, 2 * STATE), 0.5, 3.0, ((1, 32),))
    conv_bc_b = noise(keys[14], (2 * STATE,), 0.5, 3.0, ((0, 32),))
    a_log = jnp.clip(-4.0 + 4.5 * jax.random.uniform(keys[15], (MHEADS,), jnp.float32) ** levels(keys[15], (MHEADS,), ((0, 2),), -0.2, 0.2), -4.0, 0.5)
    dt_bias = jnp.clip(-6.0 + 4.0 * jax.random.uniform(keys[16], (MHEADS,), jnp.float32) ** levels(keys[16], (MHEADS,), ((0, 2),), -0.2, 0.2), -6.0, -2.0)
    d_skip = jnp.clip(0.5 + 1.0 * jax.random.uniform(keys[17], (MHEADS,), jnp.float32) ** levels(keys[17], (MHEADS,), ((0, 2),), -0.2, 0.2), 0.5, 1.5)
    w_o = noise(keys[18], (QHEADS * HEAD_DIM, D), (QHEADS * HEAD_DIM // 16) ** -0.5, 1.0, ((0, 2), (1, 16)))
    w_out = noise(keys[19], (DSSM, D), DSSM ** -0.5, 0.15625, ((0, 2), (1, 16)))
    norm2_gain = jnp.clip(1.0 + 0.1 * jax.random.normal(keys[20], (D,), jnp.float32), 0.5, 1.5).astype(jnp.bfloat16)
    w_gate = noise(keys[21], (D, FF), D ** -0.5, 0.1875, ((0, 16), (1, 2)))
    w_up = noise(keys[22], (D, FF), D ** -0.5, 0.1875, ((0, 16), (1, 2)))
    w_down = noise(keys[23], (FF, D), (FF // 4) ** -0.5, 0.25, ((0, 2), (1, 16)))
    return dict(x_in=x_in, cotangent=cotangent, positions=positions, norm1_gain=norm1_gain, w_z=w_z, w_x=w_x, w_dt=w_dt, w_q=w_q, w_k=w_k, w_v=w_v, w_bc=w_bc, conv_x_w=conv_x_w, conv_x_b=conv_x_b, conv_bc_w=conv_bc_w, conv_bc_b=conv_bc_b, a_log=a_log, dt_bias=dt_bias, d_skip=d_skip, w_o=w_o, w_out=w_out, norm2_gain=norm2_gain, w_gate=w_gate, w_up=w_up, w_down=w_down)


epsilon = 1e-05
rope_base = 100000000000.0
masked_score = -1e+30
highest = lax.Precision.HIGHEST

@jax.custom_vjp
def low(v):
    return lax.optimization_barrier(v.astype(jnp.bfloat16)).astype(jnp.float32)

@jax.custom_vjp
def low_back(v):
    return v

def low_keep(v):
    return (low(v), None)

def low_pass(kept, grad):
    return (grad,)

def back_keep(v):
    return (v, None)

def back_low(kept, grad):
    return (low(grad),)
low.defvjp(low_keep, low_pass)
low_back.defvjp(back_keep, back_low)

def full_dot(left_side, right_side):
    return jnp.dot(left_side, right_side, precision=highest)

def rms_norm(values, gain):
    return values * lax.rsqrt(lax.optimization_barrier(jnp.mean(values * values, axis=-1, keepdims=True)) + epsilon) * gain

def allowed_pairs(positions):
    row_count = positions.shape[0]
    row_index = jnp.arange(row_count, dtype=jnp.int32)[:, None]
    col_index = jnp.arange(row_count, dtype=jnp.int32)[None, :]
    reach_back = jnp.maximum(positions, 0)[:, None]
    return (col_index <= row_index) & (col_index >= row_index - reach_back)

def causal_conv(values, weight, conv_bias, positions):
    reach_back = jnp.maximum(positions, 0)[:, None]
    result = conv_bias[None, :] + weight[0][None, :] * values
    for tap_shift in range(1, weight.shape[0]):
        moved = jnp.concatenate([jnp.zeros((tap_shift, values.shape[1]), values.dtype), values[:-tap_shift]], axis=0)
        result = result + jnp.where(tap_shift <= reach_back, weight[tap_shift][None, :] * moved, 0.0)
    return result

def rotary_tables(positions, head_width):
    half_width = head_width // 2
    frequency = jnp.exp(jnp.arange(half_width, dtype=jnp.float32) * (-2.0 * math.log(rope_base) / head_width))
    angles = jnp.maximum(positions, 0).astype(jnp.float32)[:, None] * frequency[None, :]
    return (jnp.cos(angles), jnp.sin(angles))

def rotate(values, cosine, sine):
    half_width = values.shape[-1] // 2
    front_half = values[..., :half_width]
    back_half = values[..., half_width:]
    cos_rows = cosine[:, None, :]
    sin_rows = sine[:, None, :]
    return jnp.concatenate([front_half * cos_rows - back_half * sin_rows, back_half * cos_rows + front_half * sin_rows], axis=-1)

def column_part(matrix, half_index):
    part_width = matrix.shape[-1] // N_MP
    return matrix[..., half_index * part_width:(half_index + 1) * part_width]

def row_part(matrix, half_index):
    part_height = matrix.shape[0] // N_MP
    return matrix[half_index * part_height:(half_index + 1) * part_height]

def mixer_half(half_index, normed, params, positions, allowed, cosine, sine):
    norm1_gain, w_z, w_x, w_dt, w_q, w_k, w_v, w_bc, conv_x_w, conv_x_b, conv_bc_w, conv_bc_b, a_log, dt_bias, d_skip, w_o, w_out, norm2_gain, w_gate, w_up, w_down = params
    row_count = normed.shape[0]
    own_input = normed
    z_proj = low_back(full_dot(own_input, column_part(w_z, half_index)))
    x_proj = low_back(full_dot(own_input, column_part(w_x, half_index)))
    dt_proj = low_back(full_dot(own_input, column_part(w_dt, half_index)))
    q_proj = low_back(full_dot(own_input, column_part(w_q, half_index)))
    k_proj = low_back(full_dot(own_input, column_part(w_k, half_index)))
    v_proj = low_back(full_dot(own_input, column_part(w_v, half_index)))
    bc_proj = low_back(full_dot(own_input, w_bc))
    x_conv = low(jax.nn.silu(causal_conv(x_proj, column_part(conv_x_w, half_index), column_part(conv_x_b, half_index), positions)))
    bc_conv = low(jax.nn.silu(causal_conv(bc_proj, conv_bc_w, conv_bc_b, positions)))
    state_in = bc_conv[:, :STATE]
    state_out = bc_conv[:, STATE:]
    step_size = jax.nn.softplus(dt_proj + column_part(dt_bias, half_index)[None, :])
    decay_sum = jnp.cumsum(-jnp.exp(column_part(a_log, half_index))[None, :] * step_size, axis=0).T
    intersection = low_back(full_dot(state_out, state_in.T))
    decay_gap = decay_sum[:, :, None] - decay_sum[:, None, :]
    kept_decay = jnp.where(allowed[None], jnp.exp(jnp.where(allowed[None], decay_gap, 0.0)), 0.0)
    mixing = low(intersection[None] * kept_decay * step_size.T[:, None, :])
    x_heads = x_conv.reshape(row_count, -1, MHEAD_DIM)
    scan_out = jnp.einsum('hts,shp->thp', mixing, x_heads, precision=highest)
    scan_out = low_back(scan_out + column_part(d_skip, half_index)[None, :, None] * x_heads)
    gated = low((scan_out * jax.nn.silu(z_proj.reshape(row_count, -1, MHEAD_DIM))).reshape(row_count, -1))
    kv_here = KVHEADS // N_MP
    query_heads = low(rotate(q_proj.reshape(row_count, -1, HEAD_DIM), cosine, sine)).reshape(row_count, kv_here, -1, HEAD_DIM)
    key_heads = low(rotate(k_proj.reshape(row_count, kv_here, HEAD_DIM), cosine, sine))
    value_heads = low(v_proj.reshape(row_count, kv_here, HEAD_DIM))
    scores = low_back(jnp.einsum('tkgd,skd->kgts', query_heads, key_heads, precision=highest) * HEAD_DIM ** (-0.5))
    attention = jax.nn.softmax(jnp.where(allowed, scores, masked_score), axis=-1)
    attended = jnp.einsum('kgts,skd->tkgd', low(attention), value_heads, precision=highest)
    attended = low(low_back(attended)).reshape(row_count, -1)
    return full_dot(attended, row_part(w_o, half_index)) + full_dot(gated, row_part(w_out, half_index))

def block_forward(params, tokens, positions):
    norm1_gain = params[0]
    w_gate, w_up, w_down = (params[18], params[19], params[20])
    norm2_gain = params[17]
    allowed = allowed_pairs(positions)
    cosine, sine = rotary_tables(positions, HEAD_DIM)
    normed = low(rms_norm(tokens, norm1_gain))
    mixer_out = low_back(sum([mixer_half(half_index, normed, params, positions, allowed, cosine, sine) for half_index in range(N_MP)]))
    hidden_in = tokens + mixer_out
    normed2 = low(rms_norm(hidden_in, norm2_gain))
    feed_out = []
    for half_index in range(N_MP):
        own_input = normed2
        gate_value = low_back(full_dot(own_input, column_part(w_gate, half_index)))
        up_value = low_back(full_dot(own_input, column_part(w_up, half_index)))
        feed_hidden = low(jax.nn.silu(gate_value) * up_value)
        feed_out.append(full_dot(feed_hidden, row_part(w_down, half_index)))
    return hidden_in + sum(feed_out)

def reference(x_in, cotangent, positions, norm1_gain, w_z, w_x, w_dt, w_q, w_k, w_v, w_bc, conv_x_w, conv_x_b, conv_bc_w, conv_bc_b, a_log, dt_bias, d_skip, w_o, w_out, norm2_gain, w_gate, w_up, w_down):
    params = tuple((weight.astype(jnp.float32) for weight in (norm1_gain, w_z, w_x, w_dt, w_q, w_k, w_v, w_bc, conv_x_w, conv_x_b, conv_bc_w, conv_bc_b, a_log, dt_bias, d_skip, w_o, w_out, norm2_gain, w_gate, w_up, w_down)))
    buffer_count = MB * (ROWS // SLOTS)
    token_blocks = x_in.astype(jnp.float32).reshape(buffer_count, SLOTS, D)
    grad_blocks = cotangent.astype(jnp.float32).reshape(buffer_count, SLOTS, D)
    position_blocks = positions.reshape(buffer_count, SLOTS).astype(jnp.int32)

    def one_block(grad_totals, item):
        tokens, upstream, block_positions = item
        live_rows = (block_positions >= 0).astype(jnp.float32)[:, None]
        output, pull = jax.vjp(lambda weights, inputs: block_forward(weights, inputs, block_positions), params, tokens)
        weight_grads, input_grad = pull(upstream * live_rows)
        summed = tuple((running + added for running, added in zip(grad_totals, weight_grads)))
        return (summed, (output, input_grad))
    zero_grads = tuple((jnp.zeros(weight.shape, jnp.float32) for weight in params))
    grad_totals, (outputs, input_grads) = lax.scan(one_block, zero_grads, (token_blocks, grad_blocks, position_blocks))
    g_norm1_gain, g_w_z, g_w_x, g_w_dt, g_w_q, g_w_k, g_w_v, g_w_bc, g_conv_x_w, g_conv_x_b, g_conv_bc_w, g_conv_bc_b, g_a_log, g_dt_bias, g_d_skip, g_w_o, g_w_out, g_norm2_gain, g_w_gate, g_w_up, g_w_down = grad_totals
    return (outputs.reshape(MB, ROWS, D), input_grads.reshape(MB, ROWS, D), g_norm1_gain, g_w_z, g_w_x, g_w_dt, g_w_q, g_w_k, g_w_v, g_w_bc, g_conv_x_w, g_conv_x_b, g_conv_bc_w, g_conv_bc_b, g_a_log, g_dt_bias, g_d_skip, g_w_o, g_w_out, g_norm2_gain, g_w_gate, g_w_up, g_w_down)
```

```python
import math

import jax
import jax.numpy as jnp
from jax import lax
from jax.sharding import PartitionSpec as P

MHEAD_DIM = 64
STATE = 128
HEAD_DIM = 64


epsilon = 1e-05
rope_base = 100000000000.0
masked_score = -1e30
row_block = 512


def project(inputs, weight):
    return jnp.dot(inputs, weight, preferred_element_type=jnp.float32)


def weight_grad(inputs, grads):
    return jnp.einsum("ti,tj->ij", inputs, grads, preferred_element_type=jnp.float32)


def back_project(grads, weight):
    return jnp.einsum("tj,ij->ti", grads, weight, preferred_element_type=jnp.float32)


def rms_norm(values, gain):
    return values * lax.rsqrt(jnp.mean(values * values, axis=-1, keepdims=True) + epsilon) * gain


def allowed_pairs(positions, row_start, row_end):
    row_index = jnp.arange(row_start, row_end, dtype=jnp.int32)[:, None]
    col_index = jnp.arange(row_end, dtype=jnp.int32)[None, :]
    reach_back = jnp.maximum(positions, 0)[:, None]
    return (col_index <= row_index) & (col_index >= row_index - reach_back)


def causal_conv(values, weight, conv_bias, positions):
    reach_back = jnp.maximum(positions, 0)[:, None]
    result = conv_bias[None, :] + weight[0][None, :] * values
    for tap_shift in range(1, weight.shape[0]):
        moved = jnp.concatenate(
            [jnp.zeros((tap_shift, values.shape[1]), values.dtype), values[:-tap_shift]], axis=0
        )
        result = result + jnp.where(
            tap_shift <= reach_back, weight[tap_shift][None, :] * moved, 0.0
        )
    return result


def rotary_tables(positions, head_width):
    half_width = head_width // 2
    frequency = jnp.exp(
        jnp.arange(half_width, dtype=jnp.float32) * (-2.0 * math.log(rope_base) / head_width)
    )
    angles = jnp.maximum(positions, 0).astype(jnp.float32)[:, None] * frequency[None, :]
    return (jnp.cos(angles), jnp.sin(angles))


def rotate(values, cosine, sine, direction):
    half_width = values.shape[-1] // 2
    front_half = values[..., :half_width]
    back_half = values[..., half_width:]
    cos_rows = cosine[:, None, :]
    sin_rows = direction * sine[:, None, :]
    return jnp.concatenate(
        [
            front_half * cos_rows - back_half * sin_rows,
            back_half * cos_rows + front_half * sin_rows,
        ],
        axis=-1,
    )


def ssd_terms(state_in, state_out, decay_sum, step_rows, positions, row_start, row_end):
    allowed = allowed_pairs(positions, row_start, row_end)
    intersection = jnp.einsum("tn,sn->ts", state_out, state_in, preferred_element_type=jnp.float32)
    decay_gap = decay_sum[:, row_start:row_end, None] - decay_sum[:, None, :row_end]
    kept_decay = jnp.where(allowed[None], jnp.exp(jnp.where(allowed[None], decay_gap, 0.0)), 0.0)
    mixing_raw = intersection[None] * kept_decay * step_rows[:, None, :row_end]
    return (intersection, kept_decay, mixing_raw)


def attention_scores(query_heads, key_heads, positions, row_start, row_end):
    allowed = allowed_pairs(positions, row_start, row_end)
    scores = jnp.einsum(
        "tkgd,skd->kgts", query_heads, key_heads, preferred_element_type=jnp.float32
    )
    return jnp.where(allowed, scores * HEAD_DIM ** (-0.5), masked_score)


def chip_at(place, chips):
    place = lax.rem(place + 2 * chips, chips)
    half = chips // 2
    return jnp.where(place < half, 2 * place, 2 * (chips - 1 - place) + 1)


def place_of(chip, chips):
    row = chip // 2
    return jnp.where(lax.rem(chip, 2) == 0, row, chips - 1 - row)


def ring_pairs(chips, shift):
    half = chips // 2
    order = [2 * i if i < half else 2 * (chips - 1 - i) + 1 for i in range(chips)]
    return [
        (2 * order[i] + core, 2 * order[(i + shift) % chips] + core)
        for i in range(chips)
        for core in range(2)
    ]


def pair_swap(values, axis_size):
    return lax.ppermute(values, "dp", [(i, i ^ 1) for i in range(axis_size)])


def ring_gather(shard):
    dp = lax.axis_size("dp")
    chips = dp // 2
    if chips > 16 or chips % 2:
        return lax.all_gather(shard, "dp", axis=0, tiled=True)
    rows, cols = shard.shape
    cut = cols // 256 * 128
    me = lax.axis_index("dp")
    core = lax.rem(me, 2)
    place = place_of(me // 2, chips)
    up, down = ring_pairs(chips, 1), ring_pairs(chips, -1)
    held = jnp.zeros((chips, rows, cols), shard.dtype)
    held = lax.dynamic_update_slice(held, shard[None], (me // 2, 0, 0))
    ahead = behind = shard
    for step in range(1, chips // 2):
        ahead = lax.ppermute(ahead, "dp", up)
        behind = lax.ppermute(behind, "dp", down)
        held = lax.dynamic_update_slice(held, ahead[None], (chip_at(place - step, chips), 0, 0))
        held = lax.dynamic_update_slice(held, behind[None], (chip_at(place + step, chips), 0, 0))
    far = chip_at(place + chips // 2, chips)
    ahead = lax.ppermute(ahead[:, :cut], "dp", up)
    behind = lax.ppermute(behind[:, cut:], "dp", down)
    held = lax.dynamic_update_slice(held, ahead[None], (far, 0, 0))
    held = lax.dynamic_update_slice(held, behind[None], (far, 0, cut))
    other = pair_swap(held, dp)
    first = jnp.where(core == 0, held, other)
    second = jnp.where(core == 0, other, held)
    return jnp.stack([first, second], axis=1).reshape(dp * rows, cols)


def ring_scatter(total):
    dp = lax.axis_size("dp")
    chips = dp // 2
    if chips > 16 or chips % 2:
        return lax.psum_scatter(total, "dp", scatter_dimension=0, tiled=True)
    rows, cols = total.shape[0] // dp, total.shape[1]
    cut = cols // 256 * 128
    me = lax.axis_index("dp")
    core = lax.rem(me, 2)
    place = place_of(me // 2, chips)
    up, down = ring_pairs(chips, 1), ring_pairs(chips, -1)
    low = total.astype(jnp.bfloat16).reshape(chips, 2, rows, cols)
    sent = lax.dynamic_slice(low, (0, 1 - core, 0, 0), (chips, 1, rows, cols))[:, 0]
    kept = lax.dynamic_slice(low, (0, core, 0, 0), (chips, 1, rows, cols))[:, 0]
    both = (kept.astype(jnp.float32) + pair_swap(sent, dp).astype(jnp.float32)).astype(jnp.bfloat16)

    def piece(where):
        return lax.dynamic_slice(both, (chip_at(where, chips), 0, 0), (1, rows, cols))[0]

    far = piece(place + chips // 2)
    ahead = jnp.pad(lax.ppermute(far[:, :cut], "dp", up), ((0, 0), (0, cols - cut)))
    behind = jnp.pad(lax.ppermute(far[:, cut:], "dp", down), ((0, 0), (cut, 0)))
    for step in range(chips // 2 - 1, 0, -1):
        ahead = piece(place + step).astype(jnp.float32) + ahead.astype(jnp.float32)
        behind = piece(place - step).astype(jnp.float32) + behind.astype(jnp.float32)
        ahead = lax.ppermute(ahead.astype(jnp.bfloat16), "dp", up)
        behind = lax.ppermute(behind.astype(jnp.bfloat16), "dp", down)
    return (
        piece(place).astype(jnp.float32)
        + ahead.astype(jnp.float32)
        + behind.astype(jnp.float32)
    )


def swap_halves(values):
    return lax.ppermute(values, "mp", [(0, 1), (1, 0)])


def sum_halves(values):
    rounded = lax.reduce_precision(values, 8, 7)
    return rounded + swap_halves(rounded.astype(jnp.bfloat16)).astype(jnp.float32)


def forward_mixer(weights, local_params, tokens, positions):
    conv_x_w, conv_x_b, a_log, dt_bias, d_skip = local_params
    w_in = weights["in"]
    slot_count = tokens.shape[0]
    inner = conv_x_b.shape[0]
    block_rows = min(row_block, slot_count)
    residual = tokens.astype(jnp.float32)
    normed = rms_norm(residual, weights["norm1"]).astype(jnp.bfloat16)
    everything = project(normed, w_in)
    widths = weights["widths"]
    z_proj, x_proj, q_proj, bc_proj, k_proj, v_proj, misc = jnp.split(everything, widths, axis=1)
    dt_proj = misc[:, : a_log.shape[0]]
    x_conv = jax.nn.silu(
        causal_conv(x_proj, conv_x_w.astype(jnp.float32), conv_x_b.astype(jnp.float32), positions)
    ).astype(jnp.bfloat16)
    bc_conv = jax.nn.silu(
        causal_conv(bc_proj, weights["conv_bc_w"], weights["conv_bc_b"], positions)
    ).astype(jnp.bfloat16)
    state_in = bc_conv[:, :STATE]
    state_out = bc_conv[:, STATE:]
    step_size = jax.nn.softplus(dt_proj + dt_bias[None, :])
    decay_sum = jnp.cumsum(-jnp.exp(a_log)[None, :] * step_size, axis=0).T
    step_rows = step_size.T
    x_heads = x_conv.reshape(slot_count, -1, MHEAD_DIM)
    intersection, kept_decay, mixing_raw = ssd_terms(
        state_in, state_out, decay_sum, step_rows, positions, 0, block_rows
    )
    scan_rows = jnp.einsum(
        "hts,shp->thp", mixing_raw.astype(jnp.bfloat16), x_heads, preferred_element_type=jnp.float32
    )
    scan_out = scan_rows + d_skip[None, :, None] * x_heads.astype(jnp.float32)
    gated = (
        (scan_out * jax.nn.silu(z_proj.reshape(scan_out.shape)))
        .reshape(slot_count, -1)
        .astype(jnp.bfloat16)
    )
    cosine, sine = rotary_tables(positions, HEAD_DIM)
    kv_here = k_proj.shape[1] // HEAD_DIM
    query_heads = (
        rotate(q_proj.reshape(slot_count, -1, HEAD_DIM), cosine, sine, 1.0)
        .astype(jnp.bfloat16)
        .reshape(slot_count, kv_here, -1, HEAD_DIM)
    )
    key_heads = rotate(k_proj.reshape(slot_count, kv_here, HEAD_DIM), cosine, sine, 1.0).astype(
        jnp.bfloat16
    )
    value_heads = v_proj.reshape(slot_count, kv_here, HEAD_DIM).astype(jnp.bfloat16)
    scores = attention_scores(query_heads, key_heads, positions, 0, block_rows)
    row_peak = jnp.max(scores, axis=-1, keepdims=True)
    exp_scores = jnp.exp(scores - row_peak)
    row_total = jnp.sum(exp_scores, axis=-1, keepdims=True)
    attention = (exp_scores / row_total).astype(jnp.bfloat16)
    attended_rows = jnp.einsum(
        "kgts,skd->tkgd", attention, value_heads, preferred_element_type=jnp.float32
    )
    total_rows = row_peak + jnp.log(row_total)
    attended = attended_rows.reshape(slot_count, -1).astype(jnp.bfloat16)
    mixed = jnp.concatenate([attended, gated], axis=1)
    stored = {
        "residual": residual,
        "normed": normed,
        "z_proj": z_proj,
        "x_proj": x_proj,
        "dt_proj": dt_proj,
        "bc_proj": bc_proj,
        "x_conv": x_conv,
        "state_in": state_in,
        "state_out": state_out,
        "decay_sum": decay_sum,
        "step_rows": step_rows,
        "scan_out": scan_out,
        "cosine": cosine,
        "sine": sine,
        "query_heads": query_heads,
        "key_heads": key_heads,
        "value_heads": value_heads,
        "mixed": mixed,
        "log_total": total_rows,
    }
    return stored, back_project(mixed, weights["mix"])


def forward_feed(weights, stored, mixer_out):
    hidden_in = stored["residual"] + mixer_out
    normed2 = rms_norm(hidden_in, weights["norm2"]).astype(jnp.bfloat16)
    both = project(normed2, weights["feed"])
    units = both.shape[1] // 2
    gate_value, up_value = both[:, :units], both[:, units:]
    feed_hidden = (jax.nn.silu(gate_value) * up_value).astype(jnp.bfloat16)
    stored["hidden_in"] = hidden_in
    stored["normed2"] = normed2
    stored["gate_value"] = gate_value
    stored["up_value"] = up_value
    stored["feed_hidden"] = feed_hidden
    return back_project(feed_hidden, weights["down"])


def backward_feed(weights, stored, cotangent, positions):
    live_rows = (positions >= 0).astype(jnp.float32)[:, None]
    upstream = cotangent.astype(jnp.float32) * live_rows
    upstream_low = upstream.astype(jnp.bfloat16)
    d_feed_hidden = project(upstream_low, weights["down"])
    gate_value = stored["gate_value"]
    gate_sigmoid = jax.nn.sigmoid(gate_value)
    d_gate = (
        d_feed_hidden
        * stored["up_value"]
        * gate_sigmoid
        * (1.0 + gate_value * (1.0 - gate_sigmoid))
    ).astype(jnp.bfloat16)
    d_up = (d_feed_hidden * gate_value * gate_sigmoid).astype(jnp.bfloat16)
    d_both = jnp.concatenate([d_gate, d_up], axis=1)
    stored["upstream"] = upstream
    stored["upstream_low"] = upstream_low
    stored["d_both"] = d_both
    return back_project(d_both, weights["feed"])


def backward_mixer(weights, local_params, stored, d_normed2, positions):
    conv_x_w, conv_x_b, a_log, dt_bias, d_skip = local_params
    upstream = stored["upstream"]
    slot_count = upstream.shape[0]
    block_rows = min(row_block, slot_count)
    _, norm2_pull = jax.vjp(rms_norm, stored["hidden_in"], weights["norm2"])
    d_hidden_norm, grad_norm2 = norm2_pull(d_normed2)
    d_hidden = upstream + d_hidden_norm
    d_mixer = d_hidden.astype(jnp.bfloat16)
    query_heads = stored["query_heads"]
    key_heads = stored["key_heads"]
    value_heads = stored["value_heads"]
    d_mixed = project(d_mixer, weights["mix"])
    att_width = d_mixed.shape[1] - conv_x_b.shape[0]
    d_attended = d_mixed[:, :att_width].astype(jnp.bfloat16).reshape(query_heads.shape)
    z_heads = stored["z_proj"].reshape(slot_count, -1, MHEAD_DIM)
    z_sigmoid = jax.nn.sigmoid(z_heads)
    d_gated = d_mixed[:, att_width:].reshape(z_heads.shape)
    d_scan = (d_gated * z_heads * z_sigmoid).astype(jnp.bfloat16)
    d_z = (
        (d_gated * stored["scan_out"] * z_sigmoid * (1.0 + z_heads * (1.0 - z_sigmoid)))
        .reshape(slot_count, -1)
        .astype(jnp.bfloat16)
    )
    x_heads = stored["x_conv"].reshape(slot_count, -1, MHEAD_DIM)
    d_scan_wide = d_scan.astype(jnp.float32)
    grad_skip = jnp.sum(d_scan_wide * x_heads.astype(jnp.float32), axis=(0, 2))
    d_xconv = d_skip[None, :, None] * d_scan_wide
    state_in = stored["state_in"]
    state_out = stored["state_out"]
    decay_sum = stored["decay_sum"]
    step_rows = stored["step_rows"]
    d_decay = jnp.zeros(decay_sum.shape, jnp.float32)
    d_step = jnp.zeros(decay_sum.shape, jnp.float32)
    d_state_in = jnp.zeros(state_in.shape, jnp.float32)
    row_start = 0
    row_end = row_start + block_rows
    intersection, kept_decay, mixing_raw = ssd_terms(
        state_in, state_out, decay_sum, step_rows, positions, row_start, row_end
    )
    d_mixing = jnp.einsum("thp,shp->hts", d_scan, x_heads, preferred_element_type=jnp.float32)
    d_xconv = d_xconv.at[:row_end].add(
        jnp.einsum(
            "hts,thp->shp",
            mixing_raw.astype(jnp.bfloat16),
            d_scan,
            preferred_element_type=jnp.float32,
        )
    )
    pair_grad = d_mixing * mixing_raw
    d_decay = d_decay.at[:, row_start:row_end].add(jnp.sum(pair_grad, axis=2))
    d_decay = d_decay.at[:, :row_end].add(-jnp.sum(pair_grad, axis=1))
    weighted = d_mixing * kept_decay
    d_step = d_step.at[:, :row_end].add(jnp.sum(weighted * intersection[None], axis=1))
    d_intersection = jnp.sum(weighted * step_rows[:, None, :row_end], axis=0).astype(jnp.bfloat16)
    out_rows = jnp.einsum("ts,sn->tn", d_intersection, state_in, preferred_element_type=jnp.float32)
    d_state_in = d_state_in.at[:row_end].add(
        jnp.einsum("ts,tn->sn", d_intersection, state_out, preferred_element_type=jnp.float32)
    )
    decay_rates = -jnp.exp(a_log)
    d_rate = lax.cumsum(d_decay, axis=1, reverse=True)
    grad_alog = jnp.sum(d_rate * step_rows, axis=1) * decay_rates
    d_step_all = (d_step + d_rate * decay_rates[:, None]).T
    d_dt_proj = d_step_all * jax.nn.sigmoid(stored["dt_proj"] + dt_bias[None, :])
    grad_dt_bias = jnp.sum(d_dt_proj, axis=0)
    d_dt_low = d_dt_proj.astype(jnp.bfloat16)

    def conv_branch(projected, weight, conv_bias):
        return jax.nn.silu(causal_conv(projected, weight, conv_bias, positions))

    _, conv_x_pull = jax.vjp(
        conv_branch, stored["x_proj"], conv_x_w.astype(jnp.float32), conv_x_b.astype(jnp.float32)
    )
    d_x_proj, grad_conv_x_w, grad_conv_x_b = conv_x_pull(d_xconv.reshape(slot_count, -1))
    _, conv_bc_pull = jax.vjp(
        conv_branch, stored["bc_proj"], weights["conv_bc_w"], weights["conv_bc_b"]
    )
    d_bc_proj, grad_conv_bc_w, grad_conv_bc_b = conv_bc_pull(
        jnp.concatenate([d_state_in, out_rows], axis=1)
    )
    log_total = stored["log_total"]
    d_keys = jnp.zeros(key_heads.shape, jnp.float32)
    d_values = jnp.zeros(value_heads.shape, jnp.float32)
    score_scale = HEAD_DIM ** (-0.5)
    row_start = 0
    row_end = row_start + block_rows
    scores = attention_scores(query_heads, key_heads, positions, row_start, row_end)
    attention = jnp.exp(scores - log_total)
    d_values = d_values.at[:row_end].add(
        jnp.einsum(
            "kgts,tkgd->skd",
            attention.astype(jnp.bfloat16),
            d_attended,
            preferred_element_type=jnp.float32,
        )
    )
    d_attention = jnp.einsum(
        "tkgd,skd->kgts", d_attended, value_heads, preferred_element_type=jnp.float32
    )
    inner_sum = jnp.sum(attention * d_attention, axis=-1, keepdims=True)
    d_scores = (attention * (d_attention - inner_sum)).astype(jnp.bfloat16)
    query_rows = (
        jnp.einsum("kgts,skd->tkgd", d_scores, key_heads, preferred_element_type=jnp.float32)
        * score_scale
    )
    d_keys = d_keys.at[:row_end].add(
        jnp.einsum("kgts,tkgd->skd", d_scores, query_heads, preferred_element_type=jnp.float32)
        * score_scale
    )
    cosine = stored["cosine"]
    sine = stored["sine"]
    d_queries = query_rows.reshape(slot_count, -1, HEAD_DIM)
    d_q = rotate(d_queries, cosine, sine, -1.0).reshape(slot_count, -1).astype(jnp.bfloat16)
    d_k = rotate(d_keys, cosine, sine, -1.0).reshape(slot_count, -1).astype(jnp.bfloat16)
    d_v = d_values.reshape(slot_count, -1).astype(jnp.bfloat16)
    d_x_low = d_x_proj.astype(jnp.bfloat16)
    d_bc_low = d_bc_proj.astype(jnp.bfloat16)
    width = weights["in"].shape[1]
    used = [d_z, d_x_low, d_q, d_bc_low, d_k, d_v, d_dt_low]
    spare = width - sum(part.shape[1] for part in used)
    d_all = jnp.concatenate(used + [jnp.zeros((slot_count, spare), jnp.bfloat16)], axis=1)
    stored["d_mixer"] = d_mixer
    stored["d_hidden"] = d_hidden
    stored["d_all"] = d_all
    small = (grad_norm2, grad_conv_bc_w, grad_conv_bc_b, grad_conv_x_w, grad_conv_x_b)
    return back_project(d_all, weights["in"]), small + (grad_alog, grad_dt_bias, grad_skip)


def rows_joined(stored, left, right):
    total = None
    for one in stored:
        part = weight_grad(one[left], one[right])
        total = part if total is None else total + part
    return total


def local(
    x_in,
    cotangent,
    positions,
    norm1_gain,
    w_z,
    w_x,
    w_dt,
    w_q,
    w_k,
    w_v,
    w_bc,
    conv_x_w,
    conv_x_b,
    conv_bc_w,
    conv_bc_b,
    a_log,
    dt_bias,
    d_skip,
    w_o,
    w_out,
    norm2_gain,
    w_gate,
    w_up,
    w_down,
):
    local_params = (conv_x_w, conv_x_b, a_log, dt_bias, d_skip)
    micro = range(x_in.shape[0])
    half = lax.axis_index("mp")
    dp = lax.axis_size("dp")
    me = lax.axis_index("dp")
    rows = w_z.shape[0]
    heads = a_log.shape[0]

    taps = conv_bc_w.shape[0]
    bc_cols = conv_bc_b.shape[0]
    bc_taps = jnp.concatenate([conv_bc_w, conv_bc_b[None]], axis=0).T
    mine = jnp.concatenate(
        [w_bc, jnp.pad(bc_taps, ((0, w_bc.shape[0] - bc_cols), (0, 127 - taps)))], axis=1
    )
    other = swap_halves(mine)
    low_half = jnp.where(half == 0, mine, other)
    high_half = jnp.where(half == 0, other, mine)
    bc_width = w_bc.shape[1]
    bc_rows = jnp.concatenate([low_half[:, :bc_width], high_half[:, :bc_width]], axis=0)
    tap_rows = jnp.concatenate(
        [
            low_half[:bc_cols, bc_width : bc_width + taps + 1],
            high_half[:bc_cols, bc_width : bc_width + taps + 1],
            jnp.zeros((rows - 2 * bc_cols, taps + 1), w_bc.dtype),
        ],
        axis=0,
    )
    misc = jnp.concatenate([w_dt, norm1_gain[:, None], norm2_gain[:, None], tap_rows], axis=1)
    misc = jnp.pad(misc, ((0, 0), (0, 128 - misc.shape[1])))
    parts = [w_z, w_x, w_q, bc_rows, w_k, w_v, misc]
    widths = []
    for part in parts[:-1]:
        widths.append(part.shape[1] + (widths[-1] if widths else 0))
    w_in = ring_gather(jnp.concatenate(parts, axis=1))
    mix_parts = [w_o.T, w_out.T]
    mix_width = w_o.shape[0] + w_out.shape[0]
    units = w_gate.shape[1]
    rest = ring_gather(jnp.concatenate(mix_parts + [w_gate, w_up, w_down.T], axis=1))
    extra = w_in[:, widths[-1] + heads :]
    tap_all = (
        extra[:, 2 : 3 + taps]
        .reshape(dp, rows, taps + 1)[:, : 2 * bc_cols]
        .reshape(-1, taps + 1)
        .astype(jnp.float32)
    )
    weights = {
        "in": w_in,
        "widths": widths,
        "norm1": extra[:, 0].astype(jnp.float32),
        "norm2": extra[:, 1].astype(jnp.float32),
        "conv_bc_w": tap_all[:, :taps].T,
        "conv_bc_b": tap_all[:, taps],
        "mix": rest[:, :mix_width],
        "feed": rest[:, mix_width : mix_width + 2 * units],
        "down": rest[:, mix_width + 2 * units :],
    }

    stored = []
    mixer_outs = []
    for i in micro:
        one, part = forward_mixer(weights, local_params, x_in[i], positions[i])
        stored.append(one)
        mixer_outs.append(sum_halves(part))
    feed_outs = [sum_halves(forward_feed(weights, stored[i], mixer_outs[i])) for i in micro]
    outputs = [stored[i]["hidden_in"] + feed_outs[i] for i in micro]
    d_normed2 = [
        sum_halves(backward_feed(weights, stored[i], cotangent[i], positions[i])) for i in micro
    ]
    down_grad = ring_scatter(rows_joined(stored, "upstream_low", "feed_hidden"))
    feed_grad = ring_scatter(rows_joined(stored, "normed2", "d_both"))
    d_normed = []
    smalls = []
    for i in micro:
        part, small = backward_mixer(weights, local_params, stored[i], d_normed2[i], positions[i])
        d_normed.append(sum_halves(part))
        smalls.append(small)
    mix_grad = ring_scatter(rows_joined(stored, "d_mixer", "mixed"))
    in_grad = ring_scatter(rows_joined(stored, "normed", "d_all"))
    input_grads = []
    norm1_grads = []
    for i in micro:
        _, norm1_pull = jax.vjp(rms_norm, stored[i]["residual"], weights["norm1"])
        d_residual, grad_norm1 = norm1_pull(d_normed[i])
        input_grads.append(stored[i]["d_hidden"] + d_residual)
        norm1_grads.append(grad_norm1)
    packed = [(norm1_grads[i],) + smalls[i] for i in micro]
    shapes = [part.shape for part in packed[0]]
    flat = sum(jnp.concatenate([part.reshape(-1) for part in one]) for one in packed)
    flat = lax.psum(flat, "dp")
    pieces = []
    start = 0
    for shape in shapes:
        size = math.prod(shape)
        pieces.append(flat[start : start + size].reshape(shape))
        start += size
    s_norm1, s_norm2, s_bc_w, s_bc_b, g_conv_x_w, g_conv_x_b, g_alog, g_dt_bias, g_skip = pieces
    g_norm1 = lax.dynamic_slice(s_norm1, (me * rows,), (rows,))
    g_norm2 = lax.dynamic_slice(s_norm2, (me * rows,), (rows,))

    g_z, g_x, g_q, bc_grad, g_k, g_v, misc_grad = jnp.split(in_grad, widths, axis=1)
    g_dt = misc_grad[:, :heads]
    bc_kept = lax.dynamic_slice(bc_grad, (half * (rows // 2), 0), (rows // 2, bc_width))
    bc_sent = lax.dynamic_slice(bc_grad, ((1 - half) * (rows // 2), 0), (rows // 2, bc_width))
    g_bc = bc_kept + swap_halves(bc_sent)
    both_taps = jnp.concatenate([s_bc_w, s_bc_b[None]], axis=0)
    both_taps = both_taps + swap_halves(both_taps)
    my_taps = lax.dynamic_slice(
        both_taps, (0, (2 * me + half) * bc_cols), (taps + 1, bc_cols)
    )
    att_rows = w_o.shape[0]
    return (
        jnp.stack(outputs, axis=0),
        jnp.stack(input_grads, axis=0),
        g_norm1,
        g_z,
        g_x,
        g_dt,
        g_q,
        g_k,
        g_v,
        g_bc,
        g_conv_x_w,
        g_conv_x_b,
        my_taps[:taps],
        my_taps[taps],
        g_alog,
        g_dt_bias,
        g_skip,
        mix_grad[:, :att_rows].T,
        mix_grad[:, att_rows:].T,
        g_norm2,
        feed_grad[:, :units],
        feed_grad[:, units:],
        down_grad.T,
    )


def solution(mesh):
    placed = (
        P(None, "dp", None),
        P(None, "dp", None),
        P(None, "dp"),
        P("dp"),
        P("dp", "mp"),
        P("dp", "mp"),
        P("dp", "mp"),
        P("dp", "mp"),
        P("dp", "mp"),
        P("dp", "mp"),
        P(("dp", "mp"), None),
        P(None, "mp"),
        P("mp"),
        P(None, ("dp", "mp")),
        P(("dp", "mp")),
        P("mp"),
        P("mp"),
        P("mp"),
        P("mp", "dp"),
        P("mp", "dp"),
        P("dp"),
        P("dp", "mp"),
        P("dp", "mp"),
        P("mp", "dp"),
    )
    return jax.shard_map(
        local,
        mesh=mesh,
        in_specs=placed,
        out_specs=(
            P(None, "dp", None),
            P(None, "dp", None),
            P("dp"),
            P("dp", "mp"),
            P("dp", "mp"),
            P("dp", "mp"),
            P("dp", "mp"),
            P("dp", "mp"),
            P("dp", "mp"),
            P(("dp", "mp"), None),
            P(None, "mp"),
            P("mp"),
            P(None, ("dp", "mp")),
            P(("dp", "mp")),
            P("mp"),
            P("mp"),
            P("mp"),
            P("mp", "dp"),
            P("mp", "dp"),
            P("dp"),
            P("dp", "mp"),
            P("dp", "mp"),
            P("mp", "dp"),
        ),
        check_vma=False,
    )
```

```python
import math

import jax
import jax.numpy as jnp
from jax import lax
from jax.sharding import PartitionSpec as P

MHEAD_DIM = 64
STATE = 128
HEAD_DIM = 64


epsilon = 1e-05
rope_base = 100000000000.0
masked_score = -1e30
row_block = 512


def project(inputs, weight):
    return jnp.dot(inputs, weight, preferred_element_type=jnp.float32)


def weight_grad(inputs, grads):
    return jnp.einsum("ti,tj->ij", inputs, grads, preferred_element_type=jnp.float32)


def back_project(grads, weight):
    return jnp.einsum("tj,ij->ti", grads, weight, preferred_element_type=jnp.float32)


def rms_norm(values, gain):
    return values * lax.rsqrt(jnp.mean(values * values, axis=-1, keepdims=True) + epsilon) * gain


def allowed_pairs(positions, row_start, row_end):
    row_index = jnp.arange(row_start, row_end, dtype=jnp.int32)[:, None]
    col_index = jnp.arange(row_end, dtype=jnp.int32)[None, :]
    reach_back = jnp.maximum(positions, 0)[:, None]
    return (col_index <= row_index) & (col_index >= row_index - reach_back)


def causal_conv(values, weight, conv_bias, positions):
    reach_back = jnp.maximum(positions, 0)[:, None]
    result = conv_bias[None, :] + weight[0][None, :] * values
    for tap_shift in range(1, weight.shape[0]):
        moved = jnp.concatenate(
            [jnp.zeros((tap_shift, values.shape[1]), values.dtype), values[:-tap_shift]], axis=0
        )
        result = result + jnp.where(
            tap_shift <= reach_back, weight[tap_shift][None, :] * moved, 0.0
        )
    return result


def rotary_tables(positions, head_width):
    half_width = head_width // 2
    frequency = jnp.exp(
        jnp.arange(half_width, dtype=jnp.float32) * (-2.0 * math.log(rope_base) / head_width)
    )
    angles = jnp.maximum(positions, 0).astype(jnp.float32)[:, None] * frequency[None, :]
    return (jnp.cos(angles), jnp.sin(angles))


def rotate(values, cosine, sine, direction):
    half_width = values.shape[-1] // 2
    front_half = values[..., :half_width]
    back_half = values[..., half_width:]
    cos_rows = cosine[:, None, :]
    sin_rows = direction * sine[:, None, :]
    return jnp.concatenate(
        [
            front_half * cos_rows - back_half * sin_rows,
            back_half * cos_rows + front_half * sin_rows,
        ],
        axis=-1,
    )


def ssd_terms(state_in, state_out, decay_sum, step_rows, positions, row_start, row_end):
    allowed = allowed_pairs(positions, row_start, row_end)
    intersection = jnp.einsum("tn,sn->ts", state_out, state_in, preferred_element_type=jnp.float32)
    decay_gap = decay_sum[:, row_start:row_end, None] - decay_sum[:, None, :row_end]
    kept_decay = jnp.where(allowed[None], jnp.exp(jnp.where(allowed[None], decay_gap, 0.0)), 0.0)
    mixing_raw = intersection[None] * kept_decay * step_rows[:, None, :row_end]
    return (intersection, kept_decay, mixing_raw)


def attention_scores(query_heads, key_heads, positions, row_start, row_end):
    allowed = allowed_pairs(positions, row_start, row_end)
    scores = jnp.einsum(
        "tkgd,skd->kgts", query_heads, key_heads, preferred_element_type=jnp.float32
    )
    return jnp.where(allowed, scores * HEAD_DIM ** (-0.5), masked_score)


def chip_at(place, chips):
    place = lax.rem(place + 2 * chips, chips)
    half = chips // 2
    return jnp.where(place < half, 2 * place, 2 * (chips - 1 - place) + 1)


def place_of(chip, chips):
    row = chip // 2
    return jnp.where(lax.rem(chip, 2) == 0, row, chips - 1 - row)


def ring_pairs(chips, shift):
    half = chips // 2
    order = [2 * i if i < half else 2 * (chips - 1 - i) + 1 for i in range(chips)]
    return [
        (2 * order[i] + core, 2 * order[(i + shift) % chips] + core)
        for i in range(chips)
        for core in range(2)
    ]


def pair_swap(values, axis_size):
    return lax.ppermute(values, "dp", [(i, i ^ 1) for i in range(axis_size)])


def ring_gather(shard):
    dp = lax.axis_size("dp")
    chips = dp // 2
    if chips > 16 or chips % 2:
        return lax.all_gather(shard, "dp", axis=0, tiled=True)
    rows, cols = shard.shape
    cut = cols // 256 * 128
    me = lax.axis_index("dp")
    core = lax.rem(me, 2)
    place = place_of(me // 2, chips)
    up, down = ring_pairs(chips, 1), ring_pairs(chips, -1)
    held = jnp.zeros((chips, rows, cols), shard.dtype)
    held = lax.dynamic_update_slice(held, shard[None], (me // 2, 0, 0))
    ahead = behind = shard
    for step in range(1, chips // 2):
        ahead = lax.ppermute(ahead, "dp", up)
        behind = lax.ppermute(behind, "dp", down)
        held = lax.dynamic_update_slice(held, ahead[None], (chip_at(place - step, chips), 0, 0))
        held = lax.dynamic_update_slice(held, behind[None], (chip_at(place + step, chips), 0, 0))
    far = chip_at(place + chips // 2, chips)
    ahead = lax.ppermute(ahead[:, :cut], "dp", up)
    behind = lax.ppermute(behind[:, cut:], "dp", down)
    held = lax.dynamic_update_slice(held, ahead[None], (far, 0, 0))
    held = lax.dynamic_update_slice(held, behind[None], (far, 0, cut))
    other = pair_swap(held, dp)
    first = jnp.where(core == 0, held, other)
    second = jnp.where(core == 0, other, held)
    return jnp.stack([first, second], axis=1).reshape(dp * rows, cols)


def ring_scatter(total):
    dp = lax.axis_size("dp")
    chips = dp // 2
    if chips > 16 or chips % 2:
        return lax.psum_scatter(total, "dp", scatter_dimension=0, tiled=True)
    rows, cols = total.shape[0] // dp, total.shape[1]
    cut = cols // 256 * 128
    me = lax.axis_index("dp")
    core = lax.rem(me, 2)
    place = place_of(me // 2, chips)
    up, down = ring_pairs(chips, 1), ring_pairs(chips, -1)
    low = total.astype(jnp.bfloat16).reshape(chips, 2, rows, cols)
    sent = lax.dynamic_slice(low, (0, 1 - core, 0, 0), (chips, 1, rows, cols))[:, 0]
    kept = lax.dynamic_slice(low, (0, core, 0, 0), (chips, 1, rows, cols))[:, 0]
    both = (kept.astype(jnp.float32) + pair_swap(sent, dp).astype(jnp.float32)).astype(jnp.bfloat16)

    def piece(where):
        return lax.dynamic_slice(both, (chip_at(where, chips), 0, 0), (1, rows, cols))[0]

    far = piece(place + chips // 2)
    ahead = jnp.pad(lax.ppermute(far[:, :cut], "dp", up), ((0, 0), (0, cols - cut)))
    behind = jnp.pad(lax.ppermute(far[:, cut:], "dp", down), ((0, 0), (cut, 0)))
    for step in range(chips // 2 - 1, 0, -1):
        ahead = piece(place + step).astype(jnp.float32) + ahead.astype(jnp.float32)
        behind = piece(place - step).astype(jnp.float32) + behind.astype(jnp.float32)
        ahead = lax.ppermute(ahead.astype(jnp.bfloat16), "dp", up)
        behind = lax.ppermute(behind.astype(jnp.bfloat16), "dp", down)
    return (
        piece(place).astype(jnp.float32)
        + ahead.astype(jnp.float32)
        + behind.astype(jnp.float32)
    )


def swap_halves(values):
    return lax.ppermute(values, "mp", [(0, 1), (1, 0)])


def round_half(values):
    return lax.reduce_precision(values, 8, 7).astype(jnp.bfloat16)


def sum_halves(rounded, before):
    if before is not None:
        rounded, before = lax.optimization_barrier((rounded, before))
    other = swap_halves(rounded)
    return rounded.astype(jnp.float32) + other.astype(jnp.float32), other


def sum_over_dp(values):
    dp = lax.axis_size("dp")
    if dp & (dp - 1):
        return lax.psum(values, "dp")
    bit = 1
    while bit < dp:
        values = values + lax.ppermute(values, "dp", [(i, i ^ bit) for i in range(dp)])
        bit *= 2
    return values


def forward_mixer(weights, local_params, tokens, positions):
    conv_x_w, conv_x_b, a_log, dt_bias, d_skip = local_params
    w_in = weights["in"]
    slot_count = tokens.shape[0]
    inner = conv_x_b.shape[0]
    block_rows = min(row_block, slot_count)
    residual = tokens.astype(jnp.float32)
    normed = rms_norm(residual, weights["norm1"]).astype(jnp.bfloat16)
    everything = project(normed, w_in)
    widths = weights["widths"]
    z_proj, x_proj, q_proj, bc_proj, k_proj, v_proj, misc = jnp.split(everything, widths, axis=1)
    dt_proj = misc[:, : a_log.shape[0]]
    x_conv = jax.nn.silu(
        causal_conv(x_proj, conv_x_w.astype(jnp.float32), conv_x_b.astype(jnp.float32), positions)
    ).astype(jnp.bfloat16)
    bc_conv = jax.nn.silu(
        causal_conv(bc_proj, weights["conv_bc_w"], weights["conv_bc_b"], positions)
    ).astype(jnp.bfloat16)
    state_in = bc_conv[:, :STATE]
    state_out = bc_conv[:, STATE:]
    step_size = jax.nn.softplus(dt_proj + dt_bias[None, :])
    decay_sum = jnp.cumsum(-jnp.exp(a_log)[None, :] * step_size, axis=0).T
    step_rows = step_size.T
    x_heads = x_conv.reshape(slot_count, -1, MHEAD_DIM)
    intersection, kept_decay, mixing_raw = ssd_terms(
        state_in, state_out, decay_sum, step_rows, positions, 0, block_rows
    )
    scan_rows = jnp.einsum(
        "hts,shp->thp", mixing_raw.astype(jnp.bfloat16), x_heads, preferred_element_type=jnp.float32
    )
    scan_out = scan_rows + d_skip[None, :, None] * x_heads.astype(jnp.float32)
    gated = (
        (scan_out * jax.nn.silu(z_proj.reshape(scan_out.shape)))
        .reshape(slot_count, -1)
        .astype(jnp.bfloat16)
    )
    cosine, sine = rotary_tables(positions, HEAD_DIM)
    kv_here = k_proj.shape[1] // HEAD_DIM
    query_heads = (
        rotate(q_proj.reshape(slot_count, -1, HEAD_DIM), cosine, sine, 1.0)
        .astype(jnp.bfloat16)
        .reshape(slot_count, kv_here, -1, HEAD_DIM)
    )
    key_heads = rotate(k_proj.reshape(slot_count, kv_here, HEAD_DIM), cosine, sine, 1.0).astype(
        jnp.bfloat16
    )
    value_heads = v_proj.reshape(slot_count, kv_here, HEAD_DIM).astype(jnp.bfloat16)
    scores = attention_scores(query_heads, key_heads, positions, 0, block_rows)
    row_peak = jnp.max(scores, axis=-1, keepdims=True)
    exp_scores = jnp.exp(scores - row_peak)
    row_total = jnp.sum(exp_scores, axis=-1, keepdims=True)
    attention = (exp_scores / row_total).astype(jnp.bfloat16)
    attended_rows = jnp.einsum(
        "kgts,skd->tkgd", attention, value_heads, preferred_element_type=jnp.float32
    )
    total_rows = row_peak + jnp.log(row_total)
    attended = attended_rows.reshape(slot_count, -1).astype(jnp.bfloat16)
    mixed = jnp.concatenate([attended, gated], axis=1)
    stored = {
        "residual": residual,
        "normed": normed,
        "z_proj": z_proj,
        "x_proj": x_proj,
        "dt_proj": dt_proj,
        "bc_proj": bc_proj,
        "x_conv": x_conv,
        "state_in": state_in,
        "state_out": state_out,
        "decay_sum": decay_sum,
        "step_rows": step_rows,
        "scan_out": scan_out,
        "cosine": cosine,
        "sine": sine,
        "query_heads": query_heads,
        "key_heads": key_heads,
        "value_heads": value_heads,
        "mixed": mixed,
        "log_total": total_rows,
    }
    return stored, back_project(mixed, weights["mix"])


def forward_feed(weights, stored, mixer_out):
    hidden_in = stored["residual"] + mixer_out
    normed2 = rms_norm(hidden_in, weights["norm2"]).astype(jnp.bfloat16)
    both = project(normed2, weights["feed"])
    units = both.shape[1] // 2
    gate_value, up_value = both[:, :units], both[:, units:]
    feed_hidden = (jax.nn.silu(gate_value) * up_value).astype(jnp.bfloat16)
    stored["hidden_in"] = hidden_in
    stored["normed2"] = normed2
    stored["gate_value"] = gate_value
    stored["up_value"] = up_value
    stored["feed_hidden"] = feed_hidden
    return back_project(feed_hidden, weights["down"])


def backward_feed(weights, stored, cotangent, positions):
    live_rows = (positions >= 0).astype(jnp.float32)[:, None]
    upstream = cotangent.astype(jnp.float32) * live_rows
    upstream_low = upstream.astype(jnp.bfloat16)
    d_feed_hidden = project(upstream_low, weights["down"])
    gate_value = stored["gate_value"]
    gate_sigmoid = jax.nn.sigmoid(gate_value)
    d_gate = (
        d_feed_hidden
        * stored["up_value"]
        * gate_sigmoid
        * (1.0 + gate_value * (1.0 - gate_sigmoid))
    ).astype(jnp.bfloat16)
    d_up = (d_feed_hidden * gate_value * gate_sigmoid).astype(jnp.bfloat16)
    d_both = jnp.concatenate([d_gate, d_up], axis=1)
    stored["upstream"] = upstream
    stored["upstream_low"] = upstream_low
    stored["d_both"] = d_both
    return back_project(d_both, weights["feed"])


def backward_mixer(weights, local_params, stored, d_normed2, positions):
    conv_x_w, conv_x_b, a_log, dt_bias, d_skip = local_params
    upstream = stored["upstream"]
    slot_count = upstream.shape[0]
    block_rows = min(row_block, slot_count)
    _, norm2_pull = jax.vjp(rms_norm, stored["hidden_in"], weights["norm2"])
    d_hidden_norm, grad_norm2 = norm2_pull(d_normed2)
    d_hidden = upstream + d_hidden_norm
    d_mixer = d_hidden.astype(jnp.bfloat16)
    query_heads = stored["query_heads"]
    key_heads = stored["key_heads"]
    value_heads = stored["value_heads"]
    d_mixed = project(d_mixer, weights["mix"])
    att_width = d_mixed.shape[1] - conv_x_b.shape[0]
    d_attended = d_mixed[:, :att_width].astype(jnp.bfloat16).reshape(query_heads.shape)
    z_heads = stored["z_proj"].reshape(slot_count, -1, MHEAD_DIM)
    z_sigmoid = jax.nn.sigmoid(z_heads)
    d_gated = d_mixed[:, att_width:].reshape(z_heads.shape)
    d_scan = (d_gated * z_heads * z_sigmoid).astype(jnp.bfloat16)
    d_z = (
        (d_gated * stored["scan_out"] * z_sigmoid * (1.0 + z_heads * (1.0 - z_sigmoid)))
        .reshape(slot_count, -1)
        .astype(jnp.bfloat16)
    )
    x_heads = stored["x_conv"].reshape(slot_count, -1, MHEAD_DIM)
    d_scan_wide = d_scan.astype(jnp.float32)
    grad_skip = jnp.sum(d_scan_wide * x_heads.astype(jnp.float32), axis=(0, 2))
    d_xconv = d_skip[None, :, None] * d_scan_wide
    state_in = stored["state_in"]
    state_out = stored["state_out"]
    decay_sum = stored["decay_sum"]
    step_rows = stored["step_rows"]
    d_decay = jnp.zeros(decay_sum.shape, jnp.float32)
    d_step = jnp.zeros(decay_sum.shape, jnp.float32)
    d_state_in = jnp.zeros(state_in.shape, jnp.float32)
    row_start = 0
    row_end = row_start + block_rows
    intersection, kept_decay, mixing_raw = ssd_terms(
        state_in, state_out, decay_sum, step_rows, positions, row_start, row_end
    )
    d_mixing = jnp.einsum("thp,shp->hts", d_scan, x_heads, preferred_element_type=jnp.float32)
    d_xconv = d_xconv.at[:row_end].add(
        jnp.einsum(
            "hts,thp->shp",
            mixing_raw.astype(jnp.bfloat16),
            d_scan,
            preferred_element_type=jnp.float32,
        )
    )
    pair_grad = d_mixing * mixing_raw
    d_decay = d_decay.at[:, row_start:row_end].add(jnp.sum(pair_grad, axis=2))
    d_decay = d_decay.at[:, :row_end].add(-jnp.sum(pair_grad, axis=1))
    weighted = d_mixing * kept_decay
    d_step = d_step.at[:, :row_end].add(jnp.sum(weighted * intersection[None], axis=1))
    d_intersection = jnp.sum(weighted * step_rows[:, None, :row_end], axis=0).astype(jnp.bfloat16)
    out_rows = jnp.einsum("ts,sn->tn", d_intersection, state_in, preferred_element_type=jnp.float32)
    d_state_in = d_state_in.at[:row_end].add(
        jnp.einsum("ts,tn->sn", d_intersection, state_out, preferred_element_type=jnp.float32)
    )
    decay_rates = -jnp.exp(a_log)
    d_rate = lax.cumsum(d_decay, axis=1, reverse=True)
    grad_alog = jnp.sum(d_rate * step_rows, axis=1) * decay_rates
    d_step_all = (d_step + d_rate * decay_rates[:, None]).T
    d_dt_proj = d_step_all * jax.nn.sigmoid(stored["dt_proj"] + dt_bias[None, :])
    grad_dt_bias = jnp.sum(d_dt_proj, axis=0)
    d_dt_low = d_dt_proj.astype(jnp.bfloat16)

    def conv_branch(projected, weight, conv_bias):
        return jax.nn.silu(causal_conv(projected, weight, conv_bias, positions))

    _, conv_x_pull = jax.vjp(
        conv_branch, stored["x_proj"], conv_x_w.astype(jnp.float32), conv_x_b.astype(jnp.float32)
    )
    d_x_proj, grad_conv_x_w, grad_conv_x_b = conv_x_pull(d_xconv.reshape(slot_count, -1))
    _, conv_bc_pull = jax.vjp(
        conv_branch, stored["bc_proj"], weights["conv_bc_w"], weights["conv_bc_b"]
    )
    d_bc_proj, grad_conv_bc_w, grad_conv_bc_b = conv_bc_pull(
        jnp.concatenate([d_state_in, out_rows], axis=1)
    )
    log_total = stored["log_total"]
    d_keys = jnp.zeros(key_heads.shape, jnp.float32)
    d_values = jnp.zeros(value_heads.shape, jnp.float32)
    score_scale = HEAD_DIM ** (-0.5)
    row_start = 0
    row_end = row_start + block_rows
    scores = attention_scores(query_heads, key_heads, positions, row_start, row_end)
    attention = jnp.exp(scores - log_total)
    d_values = d_values.at[:row_end].add(
        jnp.einsum(
            "kgts,tkgd->skd",
            attention.astype(jnp.bfloat16),
            d_attended,
            preferred_element_type=jnp.float32,
        )
    )
    d_attention = jnp.einsum(
        "tkgd,skd->kgts", d_attended, value_heads, preferred_element_type=jnp.float32
    )
    inner_sum = jnp.sum(attention * d_attention, axis=-1, keepdims=True)
    d_scores = (attention * (d_attention - inner_sum)).astype(jnp.bfloat16)
    query_rows = (
        jnp.einsum("kgts,skd->tkgd", d_scores, key_heads, preferred_element_type=jnp.float32)
        * score_scale
    )
    d_keys = d_keys.at[:row_end].add(
        jnp.einsum("kgts,tkgd->skd", d_scores, query_heads, preferred_element_type=jnp.float32)
        * score_scale
    )
    cosine = stored["cosine"]
    sine = stored["sine"]
    d_queries = query_rows.reshape(slot_count, -1, HEAD_DIM)
    d_q = rotate(d_queries, cosine, sine, -1.0).reshape(slot_count, -1).astype(jnp.bfloat16)
    d_k = rotate(d_keys, cosine, sine, -1.0).reshape(slot_count, -1).astype(jnp.bfloat16)
    d_v = d_values.reshape(slot_count, -1).astype(jnp.bfloat16)
    d_x_low = d_x_proj.astype(jnp.bfloat16)
    d_bc_low = d_bc_proj.astype(jnp.bfloat16)
    width = weights["in"].shape[1]
    used = [d_z, d_x_low, d_q, d_bc_low, d_k, d_v, d_dt_low]
    spare = width - sum(part.shape[1] for part in used)
    d_all = jnp.concatenate(used + [jnp.zeros((slot_count, spare), jnp.bfloat16)], axis=1)
    stored["d_mixer"] = d_mixer
    stored["d_hidden"] = d_hidden
    stored["d_all"] = d_all
    small = (grad_norm2, grad_conv_bc_w, grad_conv_bc_b, grad_conv_x_w, grad_conv_x_b)
    return back_project(d_all, weights["in"]), small + (grad_alog, grad_dt_bias, grad_skip)


def rows_joined(stored, left, right):
    total = None
    for one in stored:
        part = weight_grad(one[left], one[right])
        total = part if total is None else total + part
    return total


def local(
    x_in,
    cotangent,
    positions,
    norm1_gain,
    w_z,
    w_x,
    w_dt,
    w_q,
    w_k,
    w_v,
    w_bc,
    conv_x_w,
    conv_x_b,
    conv_bc_w,
    conv_bc_b,
    a_log,
    dt_bias,
    d_skip,
    w_o,
    w_out,
    norm2_gain,
    w_gate,
    w_up,
    w_down,
):
    local_params = (conv_x_w, conv_x_b, a_log, dt_bias, d_skip)
    micro = range(x_in.shape[0])
    half = lax.axis_index("mp")
    dp = lax.axis_size("dp")
    me = lax.axis_index("dp")
    rows = w_z.shape[0]
    heads = a_log.shape[0]

    taps = conv_bc_w.shape[0]
    bc_cols = conv_bc_b.shape[0]
    bc_taps = jnp.concatenate([conv_bc_w, conv_bc_b[None]], axis=0).T
    mine = jnp.concatenate(
        [w_bc, jnp.pad(bc_taps, ((0, w_bc.shape[0] - bc_cols), (0, 127 - taps)))], axis=1
    )
    other = swap_halves(mine)
    low_half = jnp.where(half == 0, mine, other)
    high_half = jnp.where(half == 0, other, mine)
    bc_width = w_bc.shape[1]
    bc_rows = jnp.concatenate([low_half[:, :bc_width], high_half[:, :bc_width]], axis=0)
    tap_rows = jnp.concatenate(
        [
            low_half[:bc_cols, bc_width : bc_width + taps + 1],
            high_half[:bc_cols, bc_width : bc_width + taps + 1],
            jnp.zeros((rows - 2 * bc_cols, taps + 1), w_bc.dtype),
        ],
        axis=0,
    )
    misc = jnp.concatenate([w_dt, norm1_gain[:, None], norm2_gain[:, None], tap_rows], axis=1)
    misc = jnp.pad(misc, ((0, 0), (0, 128 - misc.shape[1])))
    parts = [w_z, w_x, w_q, bc_rows, w_k, w_v, misc]
    widths = []
    for part in parts[:-1]:
        widths.append(part.shape[1] + (widths[-1] if widths else 0))
    w_in = ring_gather(jnp.concatenate(parts, axis=1))
    mix_parts = [w_o.T, w_out.T]
    mix_width = w_o.shape[0] + w_out.shape[0]
    units = w_gate.shape[1]
    rest = jnp.concatenate(mix_parts + [w_gate, w_up, w_down.T], axis=1)
    rest, w_in = lax.optimization_barrier((rest, w_in))
    rest = ring_gather(rest)
    extra = w_in[:, widths[-1] + heads :]
    tap_all = (
        extra[:, 2 : 3 + taps]
        .reshape(dp, rows, taps + 1)[:, : 2 * bc_cols]
        .reshape(-1, taps + 1)
        .astype(jnp.float32)
    )
    weights = {
        "in": w_in,
        "widths": widths,
        "norm1": extra[:, 0].astype(jnp.float32),
        "norm2": extra[:, 1].astype(jnp.float32),
        "conv_bc_w": tap_all[:, :taps].T,
        "conv_bc_b": tap_all[:, taps],
        "mix": rest[:, :mix_width],
        "feed": rest[:, mix_width : mix_width + 2 * units],
        "down": rest[:, mix_width + 2 * units :],
    }

    stored = []
    halves = []
    for i in micro:
        tokens = x_in[i]
        if halves:
            tokens, halves[-1] = lax.optimization_barrier((tokens, halves[-1]))
        one, part = forward_mixer(weights, local_params, tokens, positions[i])
        stored.append(one)
        halves.append(round_half(part))
    last = None
    mixer_outs = []
    for i in micro:
        total, last = sum_halves(halves[i], last)
        mixer_outs.append(total)
    feed_halves = []
    d_halves = []
    for i in micro:
        feed_halves.append(round_half(forward_feed(weights, stored[i], mixer_outs[i])))
        d_halves.append(round_half(backward_feed(weights, stored[i], cotangent[i], positions[i])))
    d_normed2 = []
    for i in micro:
        total, last = sum_halves(d_halves[i], last)
        d_normed2.append(total)
    outputs = []
    for i in micro:
        total, last = sum_halves(feed_halves[i], last)
        outputs.append(stored[i]["hidden_in"] + total)
    down_grad = ring_scatter(rows_joined(stored, "upstream_low", "feed_hidden"))
    feed_grad = ring_scatter(rows_joined(stored, "normed2", "d_both"))
    d_normed = []
    smalls = []
    for i in micro:
        if i and i == len(micro) - 1:
            d_normed2[i], down_grad, feed_grad = lax.optimization_barrier(
                (d_normed2[i], down_grad, feed_grad)
            )
        part, small = backward_mixer(weights, local_params, stored[i], d_normed2[i], positions[i])
        total, last = sum_halves(round_half(part), last)
        d_normed.append(total)
        smalls.append(small)
    mix_grad = ring_scatter(rows_joined(stored, "d_mixer", "mixed"))
    stored[-1]["d_all"], mix_grad = lax.optimization_barrier((stored[-1]["d_all"], mix_grad))
    in_grad = ring_scatter(rows_joined(stored, "normed", "d_all"))
    input_grads = []
    norm1_grads = []
    for i in micro:
        _, norm1_pull = jax.vjp(rms_norm, stored[i]["residual"], weights["norm1"])
        d_residual, grad_norm1 = norm1_pull(d_normed[i])
        input_grads.append(stored[i]["d_hidden"] + d_residual)
        norm1_grads.append(grad_norm1)
    packed = [(norm1_grads[i],) + smalls[i] for i in micro]
    shapes = [part.shape for part in packed[0]]
    flat = sum(jnp.concatenate([part.reshape(-1) for part in one]) for one in packed)
    flat = sum_over_dp(flat)
    pieces = []
    start = 0
    for shape in shapes:
        size = math.prod(shape)
        pieces.append(flat[start : start + size].reshape(shape))
        start += size
    s_norm1, s_norm2, s_bc_w, s_bc_b, g_conv_x_w, g_conv_x_b, g_alog, g_dt_bias, g_skip = pieces
    g_norm1 = lax.dynamic_slice(s_norm1, (me * rows,), (rows,))
    g_norm2 = lax.dynamic_slice(s_norm2, (me * rows,), (rows,))

    g_z, g_x, g_q, bc_grad, g_k, g_v, misc_grad = jnp.split(in_grad, widths, axis=1)
    g_dt = misc_grad[:, :heads]
    bc_kept = lax.dynamic_slice(bc_grad, (half * (rows // 2), 0), (rows // 2, bc_width))
    bc_sent = lax.dynamic_slice(bc_grad, ((1 - half) * (rows // 2), 0), (rows // 2, bc_width))
    g_bc = bc_kept + swap_halves(bc_sent)
    both_taps = jnp.concatenate([s_bc_w, s_bc_b[None]], axis=0)
    both_taps = both_taps + swap_halves(both_taps)
    my_taps = lax.dynamic_slice(
        both_taps, (0, (2 * me + half) * bc_cols), (taps + 1, bc_cols)
    )
    att_rows = w_o.shape[0]
    return (
        jnp.stack(outputs, axis=0),
        jnp.stack(input_grads, axis=0),
        g_norm1,
        g_z,
        g_x,
        g_dt,
        g_q,
        g_k,
        g_v,
        g_bc,
        g_conv_x_w,
        g_conv_x_b,
        my_taps[:taps],
        my_taps[taps],
        g_alog,
        g_dt_bias,
        g_skip,
        mix_grad[:, :att_rows].T,
        mix_grad[:, att_rows:].T,
        g_norm2,
        feed_grad[:, :units],
        feed_grad[:, units:],
        down_grad.T,
    )


def solution(mesh):
    placed = (
        P(None, "dp", None),
        P(None, "dp", None),
        P(None, "dp"),
        P("dp"),
        P("dp", "mp"),
        P("dp", "mp"),
        P("dp", "mp"),
        P("dp", "mp"),
        P("dp", "mp"),
        P("dp", "mp"),
        P(("dp", "mp"), None),
        P(None, "mp"),
        P("mp"),
        P(None, ("dp", "mp")),
        P(("dp", "mp")),
        P("mp"),
        P("mp"),
        P("mp"),
        P("mp", "dp"),
        P("mp", "dp"),
        P("dp"),
        P("dp", "mp"),
        P("dp", "mp"),
        P("mp", "dp"),
    )
    return jax.shard_map(
        local,
        mesh=mesh,
        in_specs=placed,
        out_specs=(
            P(None, "dp", None),
            P(None, "dp", None),
            P("dp"),
            P("dp", "mp"),
            P("dp", "mp"),
            P("dp", "mp"),
            P("dp", "mp"),
            P("dp", "mp"),
            P("dp", "mp"),
            P(("dp", "mp"), None),
            P(None, "mp"),
            P("mp"),
            P(None, ("dp", "mp")),
            P(("dp", "mp")),
            P("mp"),
            P("mp"),
            P("mp"),
            P("mp", "dp"),
            P("mp", "dp"),
            P("dp"),
            P("dp", "mp"),
            P("dp", "mp"),
            P("mp", "dp"),
        ),
        check_vma=False,
    )
```
